32 devices in a mesh: batch: 8 (over z, x), centre: 4 (over y, core).
Axes of the slice: x: 2, y: 2, z: 4, core: 2. Of those that a mesh axis runs over, the one named last changes fastest.
Arguments:
- batch_features: float32 [4096, 768], P(('batch', 'centre')), may hold values from -1 to 1
- centre_features: float32 [2048, 768], P(('centre', 'batch')), may hold values from -1 to 1
- targets: float32 [4096, 512], P(('batch', 'centre')), may hold values from -6 to 6
- weights: float32 [2048, 512], P(('centre', 'batch')), may hold values from -1 to 1
Outputs:
- residual: float32 [4096, 512], P(('batch', 'centre'))
- update: float32 [2048, 512], P(('centre', 'batch'))
The draws below stay inside these ranges and needn't reach their ends.
All inputs are finite; a program needn't handle non-finite values.
Results may differ from the reference program's by a relative error of at most 0.000061.
Values sent between devices are 32-bit elements; how exact they have to be, the bound alone decides.
A program may use at most 64 MiB of HBM per device.

```python
import math
import jax
import jax.numpy as jnp
from jax import lax

D = 768
OUTW = 512
B_DEV = 512
C_DEV = 512
B = 4096
C = 2048
N_BATCH = 8
N_CENTRE = 4


cluster_count = 64


latent_rank = 32


def feature_rows(key, salt, count):
    shared = jax.random.fold_in(key, 7)
    key_means, key_basis, key_spread = jax.random.split(shared, 3)
    key_pick, key_latent, key_noise = jax.random.split(jax.random.fold_in(key, salt), 3)
    means = jax.random.normal(key_means, (cluster_count, D), jnp.float32)
    means = means / jnp.sqrt(jnp.sum(means * means, axis=1, keepdims=True))
    basis = jax.random.normal(key_basis, (latent_rank, D), jnp.float32) * math.sqrt(0.6 / (latent_rank * D))
    positions = jnp.arange(count, dtype=jnp.int32)
    upper = cluster_count - 48 * positions // count
    picks = jax.random.randint(key_pick, (count,), 0, upper).astype(jnp.int32)
    coeffs = jax.random.normal(key_latent, (count, latent_rank), jnp.float32)
    latent = jnp.dot(coeffs, basis, precision=lax.Precision.HIGHEST, preferred_element_type=jnp.float32)
    spread = jnp.exp(jax.random.uniform(key_spread, (cluster_count, 1), jnp.float32, math.log(0.15), math.log(1.5)))
    noise = jax.random.normal(key_noise, (count, D), jnp.float32) * math.sqrt(0.25 / D)
    raw = means[picks] + spread[picks] * (latent + noise)
    return raw / jnp.sqrt(jnp.sum(raw * raw, axis=1, keepdims=True))


def draw_batch_features(key, part):
    return feature_rows(key, 11, B)


def draw_centre_features(key, part):
    return feature_rows(key, 23, C)


def shard_levels(own_key, shape, cuts, low, top_value):
    loudness = 1.0
    for dim, shards_of in cuts:
        heights = jax.random.uniform(jax.random.fold_in(jax.random.fold_in(own_key, 6), dim), (shards_of,), jnp.float32, low / len(cuts), top_value / len(cuts))
        loudness = loudness * jnp.repeat(jnp.exp(heights), shape[dim] // shards_of).reshape((-1,) + (1,) * (len(shape) - 1 - dim))
    return loudness


def normal_values(own_key, shape, deviation, bound, cuts=(), held_as=jnp.bfloat16):
    result = deviation * jax.random.normal(own_key, shape, jnp.float32)
    if cuts:
        result = result * shard_levels(own_key, shape, cuts, -0.22, 0.18)
    return jnp.clip(result, -bound, bound).astype(held_as)


def setup_inputs(seed: int = 0) -> dict:
    arg_keys = jax.random.split(jax.random.key(seed), 5)
    batch_features = draw_batch_features(jax.random.fold_in(arg_keys[4], 71), 0)
    centre_features = draw_centre_features(jax.random.fold_in(arg_keys[4], 71), 0)
    targets = normal_values(arg_keys[2], (B, OUTW), 1.0, 6.0, ((0, 32),), jnp.float32)
    weights = normal_values(arg_keys[3], (C, OUTW), (max(C // 64, 1)) ** -0.5, 1.0, ((0, 32),), jnp.float32)
    return {"batch_features": batch_features, "centre_features": centre_features, "targets": targets, "weights": weights}


length_scale = 0.5
softening = 0.01

def kernel_matrix(left_rows, right_rows):
    left_norms = lax.optimization_barrier(jnp.sum(left_rows * left_rows, axis=1))
    right_norms = lax.optimization_barrier(jnp.sum(right_rows * right_rows, axis=1))
    inner = lax.dot_general(left_rows, right_rows, (((1,), (1,)), ((), ())), precision=lax.Precision.HIGHEST, preferred_element_type=jnp.float32)
    squared = left_norms[:, None] + right_norms[None, :] - 2.0 * inner
    return jnp.exp(-jnp.sqrt(squared + softening) / length_scale)

def reference(batch_features, centre_features, targets, weights):
    batch_blocks = batch_features.reshape(N_BATCH, B_DEV, D)
    centre_blocks = centre_features.reshape(N_CENTRE, C_DEV, D)

    def predict(block):
        return jnp.dot(kernel_matrix(block, centre_features), weights, precision=lax.Precision.HIGHEST, preferred_element_type=jnp.float32)
    pred = lax.map(predict, batch_blocks).reshape(B, OUTW)
    residual = pred - targets

    def project(block):
        return jnp.dot(kernel_matrix(block, batch_features), residual, precision=lax.Precision.HIGHEST, preferred_element_type=jnp.float32)
    gradient = lax.map(project, centre_blocks).reshape(C, OUTW)

    def correct(block):
        kernel_block = kernel_matrix(block, centre_features)
        return (lax.optimization_barrier(jnp.sum(kernel_block, axis=1)), jnp.dot(kernel_block, gradient, precision=lax.Precision.HIGHEST, preferred_element_type=jnp.float32))
    row_sums, product = lax.map(correct, centre_blocks)
    row_sums = row_sums.reshape(C)
    product = product.reshape(C, OUTW)
    step_size = 1.0 / jnp.max(row_sums)
    theta = 2.0 * step_size * gradient - step_size * step_size * product
    update = theta * (C / math.sqrt(B))
    return (residual, update)
```

```python
import functools
import math

import jax
import jax.numpy as jnp
from jax import lax
from jax.experimental import pallas as pl
from jax.experimental.pallas import tpu as pltpu
from jax.sharding import PartitionSpec as P

length_scale = 0.5
softening = 0.01
inner_count = 2
core_count = 2
chunk_count = 2
MESH = pl.DeviceIdType.MESH


def halves(value):
    high = value.astype(jnp.bfloat16)
    low = (value - high.astype(jnp.float32)).astype(jnp.bfloat16)
    return high, low


def product3(left_high, left_low, right):
    right_high, right_low = halves(right)
    dot = functools.partial(jnp.dot, preferred_element_type=jnp.float32)
    return (dot(left_high, right_low) + dot(left_low, right_high)) + dot(left_high, right_high)


def kernel_rows(left_rows, right_rows, right_norms):
    left_norms = jnp.sum(left_rows * left_rows, axis=1, keepdims=True)
    inner = lax.dot_general(
        left_rows,
        right_rows,
        (((1,), (1,)), ((), ())),
        precision=lax.Precision.HIGHEST,
        preferred_element_type=jnp.float32,
    )
    squared = left_norms + right_norms - 2.0 * inner
    return jnp.exp(-jnp.sqrt(squared + softening) / length_scale)


def step_kernel(
    batch_count, centre_count, output_scale,
    x_ref, c_ref, t_ref, w_ref, res_ref, upd_ref,
    xb, rf, cz, wz, kh, kl, kth, ktl, k2h, k2l,
    ps, pr, rg, gs, gr, zs, zr, gg, qs, qr, rss, rsr, ms, mrb, mrc, mrz,
    send_sem, recv_sem,
):
    outer_count = batch_count // inner_count
    side_count = centre_count // core_count
    chip_count = inner_count * side_count
    batch_place = lax.axis_index("batch")
    centre_place = lax.axis_index("centre")
    outer, inner = batch_place // inner_count, batch_place % inner_count
    side, core = centre_place // core_count, centre_place % core_count
    chip = inner * side_count + side
    other_core = 1 - core
    width = t_ref.shape[1]
    chunk = width // chunk_count
    own_centres = c_ref.shape[0]

    chip_offsets = list(range(1, chip_count))
    chip_peers = {}
    for offset in chip_offsets:
        to_inner = (inner + offset // side_count) % inner_count
        to_side = (side + offset % side_count) % side_count
        device = {"batch": outer * inner_count + to_inner, "centre": to_side * core_count + core}
        chip_peers[offset] = (to_inner * side_count + to_side, device)
    outer_offsets = sorted(range(1, outer_count), key=lambda d: min(d, outer_count - d))
    outer_peers = {}
    for offset in outer_offsets:
        to_outer = (outer + offset) % outer_count
        from_outer = (outer + outer_count - offset) % outer_count
        device = {"batch": to_outer * inner_count + inner, "centre": centre_place}
        outer_peers[offset] = (to_outer, from_outer, device)
    partner = {"batch": batch_place, "centre": side * core_count + other_core}

    started = []

    def send(src, dst, device):
        place = len(started)
        copy = pltpu.make_async_remote_copy(
            src_ref=src,
            dst_ref=dst,
            send_sem=send_sem.at[place],
            recv_sem=recv_sem.at[place],
            device_id=device,
            device_id_type=MESH,
        )
        copy.start()
        started.append(copy)
        return copy

    barrier = pltpu.get_barrier_semaphore()
    everyone = [p[1] for p in chip_peers.values()] + [p[2] for p in outer_peers.values()] + [partner]
    for device in everyone:
        pl.semaphore_signal(barrier, inc=1, device_id=device, device_id_type=MESH)
    pl.semaphore_wait(barrier, len(everyone))

    c_in = {d: send(c_ref, cz.at[core, outer], outer_peers[d][2]) for d in outer_offsets}
    x_in = {d: send(x_ref, xb.at[chip], chip_peers[d][1]) for d in chip_offsets}
    c_cross = [send(c_ref, cz.at[core, outer], partner)]
    w_in = {d: send(w_ref, wz.at[core, outer], outer_peers[d][2]) for d in outer_offsets}
    r_in = {d: send(c_ref, rf.at[chip], chip_peers[d][1]) for d in chip_offsets}
    w_cross = [send(w_ref, wz.at[core, outer], partner)]
    xb[chip] = x_ref[...]
    rf[chip] = c_ref[...]
    cz[core, outer] = c_ref[...]
    wz[core, outer] = w_ref[...]
    for d in outer_offsets:
        c_in[d].wait_recv()
        place = outer_peers[d][1]
        c_cross.append(send(cz.at[core, place], cz.at[core, place], partner))
    for copy in c_cross:
        copy.wait_recv()
    for d in chip_offsets:
        x_in[d].wait_recv()

    rows = xb.shape[0] * xb.shape[1]
    columns = core_count * outer_count * own_centres
    centre_rows = cz[...].reshape(columns, cz.shape[3])
    norms = jnp.sum(centre_rows * centre_rows, axis=1, keepdims=True)
    norms = jnp.transpose(jnp.broadcast_to(norms, (columns, 128)))[0:1, :]
    span = min(256, rows)
    blocks = span // xb.shape[1]
    for part in range(rows // span):
        left = xb[part * blocks:(part + 1) * blocks].reshape(span, xb.shape[2])
        tile = kernel_rows(left, centre_rows, norms)
        at = slice(part * span, (part + 1) * span)
        kh[at, :], kl[at, :] = halves(tile)
        kth[:, at], ktl[:, at] = halves(jnp.transpose(tile))

    for d in outer_offsets:
        w_in[d].wait_recv()
        place = outer_peers[d][1]
        w_cross.append(send(wz.at[core, place], wz.at[core, place], partner))
    for d in chip_offsets:
        r_in[d].wait_recv()
    own_rows = chip_count * own_centres
    centre_tile = kernel_rows(rf[...].reshape(own_rows, rf.shape[2]), centre_rows, norms)
    k2h[...], k2l[...] = halves(centre_tile)
    sums = jnp.sum(centre_tile, axis=1, keepdims=True)
    rss[...] = jnp.broadcast_to(sums, (own_rows, 128)).reshape(rss.shape)

    for copy in w_cross:
        copy.wait_recv()
    weight_rows = wz[...].reshape(columns, width)
    p_in = []
    for h in range(chunk_count):
        at = slice(h * chunk, (h + 1) * chunk)
        ps[h] = product3(kh[...], kl[...], weight_rows[:, at]).reshape(ps.shape[1:])
        p_in.append({d: send(ps.at[h, chip_peers[d][0]], pr.at[h, d - 1], chip_peers[d][1]) for d in chip_offsets})
    s_in = {d: send(rss.at[chip_peers[d][0]], rsr.at[d - 1], chip_peers[d][1]) for d in chip_offsets}

    res_in = []
    for h in range(chunk_count):
        at = slice(h * chunk, (h + 1) * chunk)
        total = ps[h, chip]
        for d in chip_offsets:
            p_in[h][d].wait_recv()
            total = total + pr[h, d - 1]
        residual = total - t_ref[:, at]
        res_ref[:, at] = residual
        rg[h, chip] = residual
        res_in.append({d: send(rg.at[h, chip], rg.at[h, chip], chip_peers[d][1]) for d in chip_offsets})

    total = rss[chip]
    for d in chip_offsets:
        s_in[d].wait_recv()
        total = total + rsr[d - 1]
    ms[0] = jnp.broadcast_to(jnp.max(total, axis=0, keepdims=True), ms.shape[1:])
    m_in = {d: send(ms.at[0], mrb.at[d - 1], chip_peers[d][1]) for d in chip_offsets}

    g_in = []
    for h in range(chunk_count):
        for d in chip_offsets:
            res_in[h][d].wait_recv()
        partial = product3(kth[...], ktl[...], rg[h].reshape(rows, chunk))
        gs[h] = partial.reshape(gs.shape[1:])
        g_in.append(send(gs.at[h, other_core], gr.at[h], partner))

    best = ms[0]
    for d in chip_offsets:
        m_in[d].wait_recv()
        best = jnp.maximum(best, mrb[d - 1])
    ms[1] = best
    mc_in = send(ms.at[1], mrc, partner)

    z_in = []
    for h in range(chunk_count):
        g_in[h].wait_recv()
        zs[h] = gs[h, core] + gr[h]
        z_in.append({d: send(zs.at[h, outer_peers[d][0]], zr.at[h, d - 1], outer_peers[d][2]) for d in outer_offsets})

    mc_in.wait_recv()
    ms[2] = jnp.maximum(ms[1], mrc[...])
    mz_in = {d: send(ms.at[2], mrz.at[d - 1], outer_peers[d][2]) for d in outer_offsets}

    gg_in, gg_cross = [], []
    for h in range(chunk_count):
        total = zs[h, outer]
        for d in outer_offsets:
            z_in[h][d].wait_recv()
            total = total + zr[h, d - 1]
        gg[h, core, outer] = total
        mine = gg.at[h, core, outer]
        gg_in.append({d: send(mine, mine, outer_peers[d][2]) for d in outer_offsets})
        gg_cross.append([send(mine, mine, partner)])

    best = ms[2]
    for d in outer_offsets:
        mz_in[d].wait_recv()
        best = jnp.maximum(best, mrz[d - 1])
    step_size = 1.0 / best[0:1, 0:1]

    q_in = []
    for h in range(chunk_count):
        for d in outer_offsets:
            gg_in[h][d].wait_recv()
            there = gg.at[h, core, outer_peers[d][1]]
            gg_cross[h].append(send(there, there, partner))
        for copy in gg_cross[h]:
            copy.wait_recv()
        part = product3(k2h[...], k2l[...], gg[h].reshape(columns, chunk))
        qs[h] = part.reshape(qs.shape[1:])
        q_in.append({d: send(qs.at[h, chip_peers[d][0]], qr.at[h, d - 1], chip_peers[d][1]) for d in chip_offsets})
    for h in range(chunk_count):
        total = qs[h, chip]
        for d in chip_offsets:
            q_in[h][d].wait_recv()
            total = total + qr[h, d - 1]
        theta = 2.0 * step_size * gg[h, core, outer] - step_size * step_size * total
        upd_ref[:, h * chunk:(h + 1) * chunk] = theta * output_scale

    for copy in started:
        copy.wait_send()


def shards(batch_features, centre_features, targets, weights):
    batch_count = lax.axis_size("batch")
    centre_count = lax.axis_size("centre")
    outer = batch_count // inner_count
    chips = inner_count * centre_count // core_count
    own_batch, depth = batch_features.shape
    own_centres, width = weights.shape
    chunk = width // chunk_count
    rows = chips * own_batch
    columns = core_count * outer * own_centres
    centre_total = own_centres * batch_count * centre_count
    batch_total = own_batch * batch_count * centre_count
    output_scale = centre_total / math.sqrt(batch_total)
    f32, bf16 = jnp.float32, jnp.bfloat16
    h = chunk_count
    copies = (
        4 * (outer - 1) + 2 * outer + 4 * (chips - 1) + 2
        + h * (3 * (chips - 1) + 2 * (outer - 1) + 1 + outer)
    )
    whole = pl.BlockSpec(memory_space=pltpu.VMEM)
    call = pl.pallas_call(
        functools.partial(step_kernel, batch_count, centre_count, output_scale),
        out_shape=(
            jax.ShapeDtypeStruct((own_batch, width), f32),
            jax.ShapeDtypeStruct((own_centres, width), f32),
        ),
        in_specs=[whole] * 4,
        out_specs=(whole, whole),
        scratch_shapes=[
            pltpu.VMEM((chips, own_batch, depth), f32),
            pltpu.VMEM((chips, own_centres, depth), f32),
            pltpu.VMEM((core_count, outer, own_centres, depth), f32),
            pltpu.VMEM((core_count, outer, own_centres, width), f32),
            pltpu.VMEM((rows, columns), bf16),
            pltpu.VMEM((rows, columns), bf16),
            pltpu.VMEM((columns, rows), bf16),
            pltpu.VMEM((columns, rows), bf16),
            pltpu.VMEM((chips * own_centres, columns), bf16),
            pltpu.VMEM((chips * own_centres, columns), bf16),
            pltpu.VMEM((h, chips, own_batch, chunk), f32),
            pltpu.VMEM((h, chips - 1, own_batch, chunk), f32),
            pltpu.VMEM((h, chips, own_batch, chunk), f32),
            pltpu.VMEM((h, core_count, outer, own_centres, chunk), f32),
            pltpu.VMEM((h, outer, own_centres, chunk), f32),
            pltpu.VMEM((h, outer, own_centres, chunk), f32),
            pltpu.VMEM((h, outer - 1, own_centres, chunk), f32),
            pltpu.VMEM((h, core_count, outer, own_centres, chunk), f32),
            pltpu.VMEM((h, chips, own_centres, chunk), f32),
            pltpu.VMEM((h, chips - 1, own_centres, chunk), f32),
            pltpu.VMEM((chips, own_centres, 128), f32),
            pltpu.VMEM((chips - 1, own_centres, 128), f32),
            pltpu.VMEM((3, 8, 128), f32),
            pltpu.VMEM((chips - 1, 8, 128), f32),
            pltpu.VMEM((8, 128), f32),
            pltpu.VMEM((outer - 1, 8, 128), f32),
            pltpu.SemaphoreType.DMA((copies,)),
            pltpu.SemaphoreType.DMA((copies,)),
        ],
        compiler_params=pltpu.CompilerParams(collective_id=0, has_side_effects=True),
        name="regression_step",
    )
    return call(batch_features, centre_features, targets, weights)


def solution(mesh):
    in_specs = (
        P(("batch", "centre"), None),
        P(("centre", "batch"), None),
        P(("batch", "centre"), None),
        P(("centre", "batch"), None),
    )
    out_specs = (P(("batch", "centre"), None), P(("centre", "batch"), None))
    return jax.shard_map(shards, mesh=mesh, in_specs=in_specs, out_specs=out_specs, check_vma=False)
```

```python
import functools
import math

import jax
import jax.numpy as jnp
from jax import lax
from jax.experimental import pallas as pl
from jax.experimental.pallas import tpu as pltpu
from jax.sharding import PartitionSpec as P

length_scale = 0.5
softening = 0.01
inner_count = 2
core_count = 2
chunk_count = 4
MESH = pl.DeviceIdType.MESH


def halves(value):
    high = value.astype(jnp.bfloat16)
    low = (value - high.astype(jnp.float32)).astype(jnp.bfloat16)
    return high, low


def product3(left_high, left_low, right):
    right_high, right_low = halves(right)
    dot = functools.partial(jnp.dot, preferred_element_type=jnp.float32)
    return (dot(left_high, right_low) + dot(left_low, right_high)) + dot(left_high, right_high)


def kernel_rows(left_rows, right_rows, right_norms):
    left_norms = jnp.sum(left_rows * left_rows, axis=1, keepdims=True)
    inner = lax.dot_general(
        left_rows,
        right_rows,
        (((1,), (1,)), ((), ())),
        precision=lax.Precision.HIGHEST,
        preferred_element_type=jnp.float32,
    )
    squared = left_norms + right_norms - 2.0 * inner
    return jnp.exp(-jnp.sqrt(squared + softening) / length_scale)


def step_kernel(
    batch_count, centre_count, output_scale,
    x_ref, c_ref, t_ref, w_ref, res_ref, upd_ref,
    xb, rf, cz, wz, kh, kl, kth, ktl, k2h, k2l,
    ps, pr, rg, gs, gr, zs, zr, gg, qs, qr, rss, rsr, ms, mrb, mrc, mrz,
    send_sem, recv_sem,
):
    outer_count = batch_count // inner_count
    side_count = centre_count // core_count
    chip_count = inner_count * side_count
    batch_place = lax.axis_index("batch")
    centre_place = lax.axis_index("centre")
    outer, inner = batch_place // inner_count, batch_place % inner_count
    side, core = centre_place // core_count, centre_place % core_count
    chip = inner * side_count + side
    other_core = 1 - core
    width = t_ref.shape[1]
    chunk = width // chunk_count
    own_centres = c_ref.shape[0]

    chip_offsets = list(range(1, chip_count))
    chip_peers = {}
    for offset in chip_offsets:
        to_inner = (inner + offset // side_count) % inner_count
        to_side = (side + offset % side_count) % side_count
        device = {"batch": outer * inner_count + to_inner, "centre": to_side * core_count + core}
        chip_peers[offset] = (to_inner * side_count + to_side, device)
    outer_offsets = sorted(range(1, outer_count), key=lambda d: min(d, outer_count - d))
    outer_peers = {}
    for offset in outer_offsets:
        to_outer = (outer + offset) % outer_count
        from_outer = (outer + outer_count - offset) % outer_count
        device = {"batch": to_outer * inner_count + inner, "centre": centre_place}
        outer_peers[offset] = (to_outer, from_outer, device)
    partner = {"batch": batch_place, "centre": side * core_count + other_core}

    started = []

    def send(src, dst, device):
        place = len(started)
        copy = pltpu.make_async_remote_copy(
            src_ref=src,
            dst_ref=dst,
            send_sem=send_sem.at[place],
            recv_sem=recv_sem.at[place],
            device_id=device,
            device_id_type=MESH,
        )
        copy.start()
        started.append(copy)
        return copy

    barrier = pltpu.get_barrier_semaphore()
    everyone = [p[1] for p in chip_peers.values()] + [p[2] for p in outer_peers.values()] + [partner]
    for device in everyone:
        pl.semaphore_signal(barrier, inc=1, device_id=device, device_id_type=MESH)
    pl.semaphore_wait(barrier, len(everyone))

    c_in = {d: send(c_ref, cz.at[core, outer], outer_peers[d][2]) for d in outer_offsets}
    x_in = {d: send(x_ref, xb.at[chip], chip_peers[d][1]) for d in chip_offsets}
    c_cross = [send(c_ref, cz.at[core, outer], partner)]
    w_in, w_cross = [], []
    for h in range(chunk_count):
        mine = w_ref.at[:, h * chunk:(h + 1) * chunk]
        w_in.append({d: send(mine, wz.at[h, core, outer], outer_peers[d][2]) for d in outer_offsets})
        w_cross.append([send(mine, wz.at[h, core, outer], partner)])
    r_in = {d: send(c_ref, rf.at[chip], chip_peers[d][1]) for d in chip_offsets}
    xb[chip] = x_ref[...]
    rf[chip] = c_ref[...]
    cz[core, outer] = c_ref[...]
    for h in range(chunk_count):
        wz[h, core, outer] = w_ref[:, h * chunk:(h + 1) * chunk]
    for d in outer_offsets:
        c_in[d].wait_recv()
        there = cz.at[core, outer_peers[d][1]]
        c_cross.append(send(there, there, partner))
    for copy in c_cross:
        copy.wait_recv()
    for d in chip_offsets:
        x_in[d].wait_recv()

    rows = xb.shape[0] * xb.shape[1]
    columns = core_count * outer_count * own_centres
    centre_rows = cz[...].reshape(columns, cz.shape[3])
    norms = jnp.sum(centre_rows * centre_rows, axis=1, keepdims=True)
    norms = jnp.transpose(jnp.broadcast_to(norms, (columns, 128)))[0:1, :]
    span = min(256, rows)
    blocks = span // xb.shape[1]
    for part in range(rows // span):
        left = xb[part * blocks:(part + 1) * blocks].reshape(span, xb.shape[2])
        tile = kernel_rows(left, centre_rows, norms)
        at = slice(part * span, (part + 1) * span)
        kh[at, :], kl[at, :] = halves(tile)
        kth[:, at], ktl[:, at] = halves(jnp.transpose(tile))

    p_in, res_in, z_in, gg_in, gg_cross, q_in, m_in = {}, {}, {}, {}, {}, {}, {}

    def predict(h):
        for d in outer_offsets:
            w_in[h][d].wait_recv()
            there = wz.at[h, core, outer_peers[d][1]]
            w_cross[h].append(send(there, there, partner))
        for copy in w_cross[h]:
            copy.wait_recv()
        ps[h] = product3(kh[...], kl[...], wz[h].reshape(columns, chunk)).reshape(ps.shape[1:])
        p_in[h] = {d: send(ps.at[h, chip_peers[d][0]], pr.at[h, d - 1], chip_peers[d][1]) for d in chip_offsets}

    def centre_kernel():
        for d in chip_offsets:
            r_in[d].wait_recv()
        own_rows = chip_count * own_centres
        tile = kernel_rows(rf[...].reshape(own_rows, rf.shape[2]), centre_rows, norms)
        k2h[...], k2l[...] = halves(tile)
        sums = jnp.sum(tile, axis=1, keepdims=True)
        rss[...] = jnp.broadcast_to(sums, (own_rows, 128)).reshape(rss.shape)
        m_in[0] = {d: send(rss.at[chip_peers[d][0]], rsr.at[d - 1], chip_peers[d][1]) for d in chip_offsets}

    def largest(stage):
        if stage == 0:
            total = rss[chip]
            for d in chip_offsets:
                m_in[0][d].wait_recv()
                total = total + rsr[d - 1]
            ms[0] = jnp.broadcast_to(jnp.max(total, axis=0, keepdims=True), ms.shape[1:])
            m_in[1] = {d: send(ms.at[0], mrb.at[d - 1], chip_peers[d][1]) for d in chip_offsets}
        elif stage == 1:
            best = ms[0]
            for d in chip_offsets:
                m_in[1][d].wait_recv()
                best = jnp.maximum(best, mrb[d - 1])
            ms[1] = best
            m_in[2] = send(ms.at[1], mrc, partner)
        elif stage == 2:
            m_in[2].wait_recv()
            ms[2] = jnp.maximum(ms[1], mrc[...])
            m_in[3] = {d: send(ms.at[2], mrz.at[d - 1], outer_peers[d][2]) for d in outer_offsets}

    def settle(h):
        at = slice(h * chunk, (h + 1) * chunk)
        total = ps[h, chip]
        for d in chip_offsets:
            p_in[h][d].wait_recv()
            total = total + pr[h, d - 1]
        residual = total - t_ref[:, at]
        res_ref[:, at] = residual
        rg[h, chip] = residual
        res_in[h] = {d: send(rg.at[h, chip], rg.at[h, chip], chip_peers[d][1]) for d in chip_offsets}

    def project(h):
        for d in chip_offsets:
            res_in[h][d].wait_recv()
        partial = product3(kth[...], ktl[...], rg[h].reshape(rows, chunk))
        gs[h] = partial.reshape(gs.shape[1:])
        crossing = send(gs.at[h, other_core], gr.at[h], partner)
        crossing.wait_recv()
        zs[h] = gs[h, core] + gr[h]
        z_in[h] = {d: send(zs.at[h, outer_peers[d][0]], zr.at[h, d - 1], outer_peers[d][2]) for d in outer_offsets}

    def gather_gradient(h):
        total = zs[h, outer]
        for d in outer_offsets:
            z_in[h][d].wait_recv()
            total = total + zr[h, d - 1]
        gg[h, core, outer] = total
        mine = gg.at[h, core, outer]
        gg_in[h] = {d: send(mine, mine, outer_peers[d][2]) for d in outer_offsets}
        gg_cross[h] = [send(mine, mine, partner)]

    def correct(h):
        for d in outer_offsets:
            gg_in[h][d].wait_recv()
            there = gg.at[h, core, outer_peers[d][1]]
            gg_cross[h].append(send(there, there, partner))
        for copy in gg_cross[h]:
            copy.wait_recv()
        part = product3(k2h[...], k2l[...], gg[h].reshape(columns, chunk))
        qs[h] = part.reshape(qs.shape[1:])
        q_in[h] = {d: send(qs.at[h, chip_peers[d][0]], qr.at[h, d - 1], chip_peers[d][1]) for d in chip_offsets}

    predict(0)
    predict(1)
    centre_kernel()
    settle(0)
    predict(2)
    largest(0)
    settle(1)
    predict(3)
    largest(1)
    project(0)
    settle(2)
    largest(2)
    project(1)
    gather_gradient(0)
    settle(3)
    project(2)
    gather_gradient(1)
    project(3)
    correct(0)
    gather_gradient(2)
    correct(1)
    gather_gradient(3)
    correct(2)
    correct(3)

    best = ms[2]
    for d in outer_offsets:
        m_in[3][d].wait_recv()
        best = jnp.maximum(best, mrz[d - 1])
    step_size = 1.0 / best[0:1, 0:1]
    for h in range(chunk_count):
        total = qs[h, chip]
        for d in chip_offsets:
            q_in[h][d].wait_recv()
            total = total + qr[h, d - 1]
        theta = 2.0 * step_size * gg[h, core, outer] - step_size * step_size * total
        upd_ref[:, h * chunk:(h + 1) * chunk] = theta * output_scale

    for copy in started:
        copy.wait_send()


def shards(batch_features, centre_features, targets, weights):
    batch_count = lax.axis_size("batch")
    centre_count = lax.axis_size("centre")
    outer = batch_count // inner_count
    chips = inner_count * centre_count // core_count
    own_batch, depth = batch_features.shape
    own_centres, width = weights.shape
    chunk = width // chunk_count
    rows = chips * own_batch
    columns = core_count * outer * own_centres
    centre_total = own_centres * batch_count * centre_count
    batch_total = own_batch * batch_count * centre_count
    output_scale = centre_total / math.sqrt(batch_total)
    f32, bf16 = jnp.float32, jnp.bfloat16
    h = chunk_count
    copies = (
        4 * (outer - 1) + 2 * outer + 4 * (chips - 1) + 2
        + h * (3 * (chips - 1) + 3 * (outer - 1) + 1 + 2 * outer)
    )
    whole = pl.BlockSpec(memory_space=pltpu.VMEM)
    call = pl.pallas_call(
        functools.partial(step_kernel, batch_count, centre_count, output_scale),
        out_shape=(
            jax.ShapeDtypeStruct((own_batch, width), f32),
            jax.ShapeDtypeStruct((own_centres, width), f32),
        ),
        in_specs=[whole] * 4,
        out_specs=(whole, whole),
        scratch_shapes=[
            pltpu.VMEM((chips, own_batch, depth), f32),
            pltpu.VMEM((chips, own_centres, depth), f32),
            pltpu.VMEM((core_count, outer, own_centres, depth), f32),
            pltpu.VMEM((h, core_count, outer, own_centres, chunk), f32),
            pltpu.VMEM((rows, columns), bf16),
            pltpu.VMEM((rows, columns), bf16),
            pltpu.VMEM((columns, rows), bf16),
            pltpu.VMEM((columns, rows), bf16),
            pltpu.VMEM((chips * own_centres, columns), bf16),
            pltpu.VMEM((chips * own_centres, columns), bf16),
            pltpu.VMEM((h, chips, own_batch, chunk), f32),
            pltpu.VMEM((h, chips - 1, own_batch, chunk), f32),
            pltpu.VMEM((h, chips, own_batch, chunk), f32),
            pltpu.VMEM((h, core_count, outer, own_centres, chunk), f32),
            pltpu.VMEM((h, outer, own_centres, chunk), f32),
            pltpu.VMEM((h, outer, own_centres, chunk), f32),
            pltpu.VMEM((h, outer - 1, own_centres, chunk), f32),
            pltpu.VMEM((h, core_count, outer, own_centres, chunk), f32),
            pltpu.VMEM((h, chips, own_centres, chunk), f32),
            pltpu.VMEM((h, chips - 1, own_centres, chunk), f32),
            pltpu.VMEM((chips, own_centres, 128), f32),
            pltpu.VMEM((chips - 1, own_centres, 128), f32),
            pltpu.VMEM((3, 8, 128), f32),
            pltpu.VMEM((chips - 1, 8, 128), f32),
            pltpu.VMEM((8, 128), f32),
            pltpu.VMEM((outer - 1, 8, 128), f32),
            pltpu.SemaphoreType.DMA((copies,)),
            pltpu.SemaphoreType.DMA((copies,)),
        ],
        compiler_params=pltpu.CompilerParams(collective_id=0, has_side_effects=True),
        name="regression_step",
    )
    return call(batch_features, centre_features, targets, weights)


def solution(mesh):
    in_specs = (
        P(("batch", "centre"), None),
        P(("centre", "batch"), None),
        P(("batch", "centre"), None),
        P(("centre", "batch"), None),
    )
    out_specs = (P(("batch", "centre"), None), P(("centre", "batch"), None))
    return jax.shard_map(shards, mesh=mesh, in_specs=in_specs, out_specs=out_specs, check_vma=False)
```

```python
import functools
import math

import jax
import jax.numpy as jnp
from jax import lax
from jax.experimental import pallas as pl
from jax.experimental.pallas import tpu as pltpu
from jax.sharding import PartitionSpec as P

length_scale = 0.5
softening = 0.01
inner_count = 2
core_count = 2
chunk_count = 4
MESH = pl.DeviceIdType.MESH


def halves(value):
    high = value.astype(jnp.bfloat16)
    low = (value - high.astype(jnp.float32)).astype(jnp.bfloat16)
    return high, low


def product3(left_high, left_low, right):
    right_high, right_low = halves(right)
    dot = functools.partial(jnp.dot, preferred_element_type=jnp.float32)
    return (dot(left_high, right_low) + dot(left_low, right_high)) + dot(left_high, right_high)


def kernel_rows(left_rows, right_rows, right_norms):
    left_norms = jnp.sum(left_rows * left_rows, axis=1, keepdims=True)
    inner = lax.dot_general(
        left_rows,
        right_rows,
        (((1,), (1,)), ((), ())),
        precision=lax.Precision.HIGHEST,
        preferred_element_type=jnp.float32,
    )
    squared = left_norms + right_norms - 2.0 * inner
    return jnp.exp(-jnp.sqrt(squared + softening) / length_scale)


def step_kernel(
    batch_count, centre_count, output_scale,
    x_ref, c_ref, t_ref, w_ref, res_ref, upd_ref,
    xb, rf, cz, wz, kh, kl, kth, ktl, k2h, k2l,
    ps, pr, rg, gs, gr, zs, zr, gg, qs, qr, rss, rsr, ms, mrb, mrc, mrz,
    send_sem, recv_sem,
):
    outer_count = batch_count // inner_count
    side_count = centre_count // core_count
    chip_count = inner_count * side_count
    batch_place = lax.axis_index("batch")
    centre_place = lax.axis_index("centre")
    outer, inner = batch_place // inner_count, batch_place % inner_count
    side, core = centre_place // core_count, centre_place % core_count
    chip = inner * side_count + side
    other_core = 1 - core
    width = t_ref.shape[1]
    chunk = width // chunk_count
    own_centres = c_ref.shape[0]

    chip_offsets = list(range(1, chip_count))
    chip_peers = {}
    for offset in chip_offsets:
        to_inner = (inner + offset // side_count) % inner_count
        to_side = (side + offset % side_count) % side_count
        device = {"batch": outer * inner_count + to_inner, "centre": to_side * core_count + core}
        chip_peers[offset] = (to_inner * side_count + to_side, device)
    outer_offsets = sorted(range(1, outer_count), key=lambda d: min(d, outer_count - d))
    outer_peers = {}
    for offset in outer_offsets:
        to_outer = (outer + offset) % outer_count
        from_outer = (outer + outer_count - offset) % outer_count
        device = {"batch": to_outer * inner_count + inner, "centre": centre_place}
        outer_peers[offset] = (to_outer, from_outer, device)
    partner = {"batch": batch_place, "centre": side * core_count + other_core}

    started = []

    def send(src, dst, device):
        place = len(started)
        copy = pltpu.make_async_remote_copy(
            src_ref=src,
            dst_ref=dst,
            send_sem=send_sem.at[place],
            recv_sem=recv_sem.at[place],
            device_id=device,
            device_id_type=MESH,
        )
        copy.start()
        started.append(copy)
        return copy

    barrier = pltpu.get_barrier_semaphore()
    everyone = [p[1] for p in chip_peers.values()] + [p[2] for p in outer_peers.values()] + [partner]
    for device in everyone:
        pl.semaphore_signal(barrier, inc=1, device_id=device, device_id_type=MESH)
    pl.semaphore_wait(barrier, len(everyone))

    c_in = {d: send(c_ref, cz.at[core, outer], outer_peers[d][2]) for d in outer_offsets}
    x_in = {d: send(x_ref, xb.at[chip], chip_peers[d][1]) for d in chip_offsets}
    c_cross = [send(c_ref, cz.at[core, outer], partner)]
    w_in, w_cross = [], []

    def send_weights(h):
        mine = w_ref.at[:, h * chunk:(h + 1) * chunk]
        w_in.append({d: send(mine, wz.at[h, core, outer], outer_peers[d][2]) for d in outer_offsets})
        w_cross.append([send(mine, wz.at[h, core, outer], partner)])

    xb[chip] = x_ref[...]
    rf[chip] = c_ref[...]
    cz[core, outer] = c_ref[...]
    for h in range(chunk_count):
        wz[h, core, outer] = w_ref[:, h * chunk:(h + 1) * chunk]
    for d in outer_offsets:
        c_in[d].wait_recv()
        there = cz.at[core, outer_peers[d][1]]
        c_cross.append(send(there, there, partner))
    send_weights(0)
    send_weights(1)
    for copy in c_cross:
        copy.wait_recv()
    for d in chip_offsets:
        x_in[d].wait_recv()
    r_in = {d: send(c_ref, rf.at[chip], chip_peers[d][1]) for d in chip_offsets}

    rows = xb.shape[0] * xb.shape[1]
    columns = core_count * outer_count * own_centres
    centre_rows = cz[...].reshape(columns, cz.shape[3])
    norms = jnp.sum(centre_rows * centre_rows, axis=1, keepdims=True)
    norms = jnp.transpose(jnp.broadcast_to(norms, (columns, 128)))[0:1, :]
    span = min(256, rows)
    blocks = span // xb.shape[1]
    for part in range(rows // span):
        left = xb[part * blocks:(part + 1) * blocks].reshape(span, xb.shape[2])
        tile = kernel_rows(left, centre_rows, norms)
        at = slice(part * span, (part + 1) * span)
        kh[at, :], kl[at, :] = halves(tile)
        kth[:, at], ktl[:, at] = halves(jnp.transpose(tile))

    for h in range(2, chunk_count):
        send_weights(h)

    p_in, res_in, z_in, gg_in, gg_cross, q_in, m_in = {}, {}, {}, {}, {}, {}, {}

    def predict(h):
        for d in outer_offsets:
            w_in[h][d].wait_recv()
            there = wz.at[h, core, outer_peers[d][1]]
            w_cross[h].append(send(there, there, partner))
        for copy in w_cross[h]:
            copy.wait_recv()
        ps[h] = product3(kh[...], kl[...], wz[h].reshape(columns, chunk)).reshape(ps.shape[1:])
        p_in[h] = {d: send(ps.at[h, chip_peers[d][0]], pr.at[h, d - 1], chip_peers[d][1]) for d in chip_offsets}

    def centre_kernel():
        for d in chip_offsets:
            r_in[d].wait_recv()
        own_rows = chip_count * own_centres
        tile = kernel_rows(rf[...].reshape(own_rows, rf.shape[2]), centre_rows, norms)
        k2h[...], k2l[...] = halves(tile)
        sums = jnp.sum(tile, axis=1, keepdims=True)
        rss[...] = jnp.broadcast_to(sums, (own_rows, 128)).reshape(rss.shape)
        m_in[0] = {d: send(rss.at[chip_peers[d][0]], rsr.at[d - 1], chip_peers[d][1]) for d in chip_offsets}

    def largest(stage):
        if stage == 0:
            total = rss[chip]
            for d in chip_offsets:
                m_in[0][d].wait_recv()
                total = total + rsr[d - 1]
            ms[0] = jnp.broadcast_to(jnp.max(total, axis=0, keepdims=True), ms.shape[1:])
            m_in[1] = {d: send(ms.at[0], mrb.at[d - 1], chip_peers[d][1]) for d in chip_offsets}
        elif stage == 1:
            best = ms[0]
            for d in chip_offsets:
                m_in[1][d].wait_recv()
                best = jnp.maximum(best, mrb[d - 1])
            ms[1] = best
            m_in[2] = send(ms.at[1], mrc, partner)
        elif stage == 2:
            m_in[2].wait_recv()
            ms[2] = jnp.maximum(ms[1], mrc[...])
            m_in[3] = {d: send(ms.at[2], mrz.at[d - 1], outer_peers[d][2]) for d in outer_offsets}

    def settle(h):
        at = slice(h * chunk, (h + 1) * chunk)
        total = ps[h, chip]
        for d in chip_offsets:
            p_in[h][d].wait_recv()
            total = total + pr[h, d - 1]
        residual = total - t_ref[:, at]
        res_ref[:, at] = residual
        rg[h, chip] = residual
        res_in[h] = {d: send(rg.at[h, chip], rg.at[h, chip], chip_peers[d][1]) for d in chip_offsets}

    def project(h):
        for d in chip_offsets:
            res_in[h][d].wait_recv()
        partial = product3(kth[...], ktl[...], rg[h].reshape(rows, chunk))
        gs[h] = partial.reshape(gs.shape[1:])
        crossing = send(gs.at[h, other_core], gr.at[h], partner)
        crossing.wait_recv()
        zs[h] = gs[h, core] + gr[h]
        z_in[h] = {d: send(zs.at[h, outer_peers[d][0]], zr.at[h, d - 1], outer_peers[d][2]) for d in outer_offsets}

    def gather_gradient(h):
        total = zs[h, outer]
        for d in outer_offsets:
            z_in[h][d].wait_recv()
            total = total + zr[h, d - 1]
        gg[h, core, outer] = total
        mine = gg.at[h, core, outer]
        gg_in[h] = {d: send(mine, mine, outer_peers[d][2]) for d in outer_offsets}
        gg_cross[h] = [send(mine, mine, partner)]

    def correct(h):
        for d in outer_offsets:
            gg_in[h][d].wait_recv()
            there = gg.at[h, core, outer_peers[d][1]]
            gg_cross[h].append(send(there, there, partner))
        for copy in gg_cross[h]:
            copy.wait_recv()
        part = product3(k2h[...], k2l[...], gg[h].reshape(columns, chunk))
        qs[h] = part.reshape(qs.shape[1:])
        q_in[h] = {d: send(qs.at[h, chip_peers[d][0]], qr.at[h, d - 1], chip_peers[d][1]) for d in chip_offsets}

    predict(0)
    predict(1)
    centre_kernel()
    settle(0)
    predict(2)
    largest(0)
    settle(1)
    predict(3)
    largest(1)
    project(0)
    settle(2)
    largest(2)
    project(1)
    gather_gradient(0)
    settle(3)
    project(2)
    gather_gradient(1)
    project(3)
    correct(0)
    gather_gradient(2)
    correct(1)
    gather_gradient(3)
    correct(2)
    correct(3)

    best = ms[2]
    for d in outer_offsets:
        m_in[3][d].wait_recv()
        best = jnp.maximum(best, mrz[d - 1])
    step_size = 1.0 / best[0:1, 0:1]
    for h in range(chunk_count):
        total = qs[h, chip]
        for d in chip_offsets:
            q_in[h][d].wait_recv()
            total = total + qr[h, d - 1]
        theta = 2.0 * step_size * gg[h, core, outer] - step_size * step_size * total
        upd_ref[:, h * chunk:(h + 1) * chunk] = theta * output_scale

    for copy in started:
        copy.wait_send()


def shards(batch_features, centre_features, targets, weights):
    batch_count = lax.axis_size("batch")
    centre_count = lax.axis_size("centre")
    outer = batch_count // inner_count
    chips = inner_count * centre_count // core_count
    own_batch, depth = batch_features.shape
    own_centres, width = weights.shape
    chunk = width // chunk_count
    rows = chips * own_batch
    columns = core_count * outer * own_centres
    centre_total = own_centres * batch_count * centre_count
    batch_total = own_batch * batch_count * centre_count
    output_scale = centre_total / math.sqrt(batch_total)
    f32, bf16 = jnp.float32, jnp.bfloat16
    h = chunk_count
    copies = (
        4 * (outer - 1) + 2 * outer + 4 * (chips - 1) + 2
        + h * (3 * (chips - 1) + 3 * (outer - 1) + 1 + 2 * outer)
    )
    whole = pl.BlockSpec(memory_space=pltpu.VMEM)
    call = pl.pallas_call(
        functools.partial(step_kernel, batch_count, centre_count, output_scale),
        out_shape=(
            jax.ShapeDtypeStruct((own_batch, width), f32),
            jax.ShapeDtypeStruct((own_centres, width), f32),
        ),
        in_specs=[whole] * 4,
        out_specs=(whole, whole),
        scratch_shapes=[
            pltpu.VMEM((chips, own_batch, depth), f32),
            pltpu.VMEM((chips, own_centres, depth), f32),
            pltpu.VMEM((core_count, outer, own_centres, depth), f32),
            pltpu.VMEM((h, core_count, outer, own_centres, chunk), f32),
            pltpu.VMEM((rows, columns), bf16),
            pltpu.VMEM((rows, columns), bf16),
            pltpu.VMEM((columns, rows), bf16),
            pltpu.VMEM((columns, rows), bf16),
            pltpu.VMEM((chips * own_centres, columns), bf16),
            pltpu.VMEM((chips * own_centres, columns), bf16),
            pltpu.VMEM((h, chips, own_batch, chunk), f32),
            pltpu.VMEM((h, chips - 1, own_batch, chunk), f32),
            pltpu.VMEM((h, chips, own_batch, chunk), f32),
            pltpu.VMEM((h, core_count, outer, own_centres, chunk), f32),
            pltpu.VMEM((h, outer, own_centres, chunk), f32),
            pltpu.VMEM((h, outer, own_centres, chunk), f32),
            pltpu.VMEM((h, outer - 1, own_centres, chunk), f32),
            pltpu.VMEM((h, core_count, outer, own_centres, chunk), f32),
            pltpu.VMEM((h, chips, own_centres, chunk), f32),
            pltpu.VMEM((h, chips - 1, own_centres, chunk), f32),
            pltpu.VMEM((chips, own_centres, 128), f32),
            pltpu.VMEM((chips - 1, own_centres, 128), f32),
            pltpu.VMEM((3, 8, 128), f32),
            pltpu.VMEM((chips - 1, 8, 128), f32),
            pltpu.VMEM((8, 128), f32),
            pltpu.VMEM((outer - 1, 8, 128), f32),
            pltpu.SemaphoreType.DMA((copies,)),
            pltpu.SemaphoreType.DMA((copies,)),
        ],
        compiler_params=pltpu.CompilerParams(collective_id=0, has_side_effects=True),
        name="regression_step",
    )
    return call(batch_features, centre_features, targets, weights)


def solution(mesh):
    in_specs = (
        P(("batch", "centre"), None),
        P(("centre", "batch"), None),
        P(("batch", "centre"), None),
        P(("centre", "batch"), None),
    )
    out_specs = (P(("batch", "centre"), None), P(("centre", "batch"), None))
    return jax.shard_map(shards, mesh=mesh, in_specs=in_specs, out_specs=out_specs, check_vma=False)
```
